128 devices in a mesh: orb: 128 (over y, x, z, core).
Axes of the slice: x: 4, y: 4, z: 4, core: 2. Of those that a mesh axis runs over, the one named last changes fastest.
Arguments:
- three_index: bfloat16 [128, 1024, 512], P('orb'), may hold values from -1 to 1
- ovl: bfloat16 [512, 512], replicated, may hold values from -1.5 to 1.6, as said below
- fock_virt: bfloat16 [512, 512], replicated, may hold values from -0.5 to 3.5, as said below
- fock_occ: float32 [128], replicated, may hold values from -1.2 to -0.4
- pair_partner: int32 [128, 4], P('orb'), may hold values from 0 to 127, as said below
- coup_pair: int32 [512, 2], P('orb'), may hold values from 0 to 511, as said below
- coup_fock: float32 [512, 2], P('orb'), may hold values from -1.2 to 1.2
- dom_blocks: int32 [512], P('orb'), may hold values from 1 to 2
Outputs:
- amplitudes: bfloat16 [512, 512, 512], P('orb')
- residual: float32 [512, 512, 512], P('orb')
- pair_energy: float32 [512], P('orb')
The draws below stay inside these ranges and needn't reach their ends.
Inputs may be any that keep to these rules, and one draw needn't show every extreme that they name: `pair_partner`: row i names 4 different orbitals j, none equal to i, each with |j - i| <= 4; the first of them is exactly 4 away. `coup_pair`: pair g belongs to orbital g // 4. The 8 entries in the rows of one orbital's pairs name pairs of as many different other orbitals, each within 8 of it in orbital order; the first entry's orbital is exactly 8 away. `ovl`: diagonal between 0.8 and 1.2, small entries off it. `fock_virt`: diagonal between 0.3 and 3, small entries off it.
All inputs are finite; a program needn't handle non-finite values.
Results may differ from the reference program's by a relative error of at most 0.012.
The reference program's roundings to bfloat16 on the way count: a program that leaves them out, or rounds other values in their place, can miss the bound.
Values may be sent and summed in bfloat16 or wider, within the bound.
No kernel may reach another device: no remote copies, remote signals or barrier semaphores. Data moves between devices by JAX's collectives and lax.ppermute only.
A program may use at most 128 MiB of HBM per device.

```python
import jax
import jax.numpy as jnp
from jax import lax

NAUX = 1024
NV = 512
COUP = 2
ITERS = 2
PAIR_DEV = 4
NOCC = 128
NPAIRS = 512
REACH = 8
BLOCK_REACH = 4


def choose_offsets(key, count, reach_span):
    orbitals = jnp.arange(NOCC, dtype=jnp.int32)[:, None]
    offsets = jnp.concatenate([jnp.arange(-reach_span, 0), jnp.arange(1, reach_span + 1)]).astype(jnp.int32)[None, :]
    targets = orbitals + offsets
    valid = (targets >= 0) & (targets < NOCC)
    width = 2 * reach_span
    columns = jnp.arange(width, dtype=jnp.int32)[None, :]
    scores = jax.random.randint(key, (NOCC, width), 0, 1 << 20) * width + columns
    extreme = jnp.where(orbitals + reach_span < NOCC, width - 1, 0)
    scores = jnp.where(columns == extreme, -1, scores)
    scores = jnp.where(valid, scores, 1 << 30)
    order = jnp.argsort(scores, axis=1, stable=True)[:, :count]
    return jnp.take_along_axis(targets, order, axis=1).astype(jnp.int32)


def draw_pair_partner(key, part):
    return choose_offsets(jax.random.fold_in(key, 11), PAIR_DEV, BLOCK_REACH)


def draw_coup_pair(key, part):
    owners = choose_offsets(jax.random.fold_in(key, 23), PAIR_DEV * COUP, REACH)
    local_slot = jax.random.randint(jax.random.fold_in(key, 29), (NOCC, PAIR_DEV * COUP), 0, PAIR_DEV)
    return (owners * PAIR_DEV + local_slot).reshape(NOCC * PAIR_DEV, COUP).astype(jnp.int32)


def draw_ovl(key, part):
    first_key, second_key = jax.random.split(key)
    diagonal = jax.random.uniform(first_key, (NV,), jnp.float32, 0.8, 1.2)
    spread = 0.5 / jnp.sqrt(jnp.float32(NV))
    offdiag = jnp.clip(jax.random.normal(second_key, (NV, NV), jnp.float32), -4.0, 4.0) * spread
    return (jnp.diag(diagonal) + offdiag).astype(jnp.bfloat16)


def draw_fock_virt(key, part):
    first_key, second_key = jax.random.split(key)
    diagonal = jnp.exp(jax.random.uniform(first_key, (NV,), jnp.float32, jnp.log(0.3), jnp.log(3.0)))
    spread = 0.4 / jnp.sqrt(jnp.float32(NV))
    offdiag = jnp.clip(jax.random.normal(second_key, (NV, NV), jnp.float32), -4.0, 4.0) * spread
    return (jnp.diag(diagonal) + offdiag).astype(jnp.bfloat16)


def place_ends(result, key, least, largest):
    spot = [jax.random.randint(jax.random.fold_in(key, axis), (), 0, length) for axis, length in enumerate(result.shape)]
    widest = result.shape.index(max(result.shape))
    beside = spot[:widest] + [(spot[widest] + 1) % result.shape[widest]] + spot[widest + 1:]
    return result.at[tuple(spot)].set(least).at[tuple(beside)].set(largest)


def block_scale(rng, shape, shards, low, high):
    def one(position, blocks):
        steps = jax.random.uniform(jax.random.fold_in(jax.random.fold_in(rng, 6), position), (blocks,), jnp.float32, low / len(shards), high / len(shards))
        return jnp.repeat(jnp.exp(steps), shape[position] // blocks).reshape((-1,) + (1,) * (len(shape) - position - 1))

    loudness = one(*shards[0])
    for cut in shards[1:]:
        loudness = loudness * one(*cut)
    return loudness


def gaussian(key, dims, scale, bound, cuts=(), kind=jnp.bfloat16):
    entries = scale * jax.random.normal(key, dims, jnp.float32)
    if cuts:
        entries = entries * block_scale(key, dims, cuts, -0.22, 0.18)
    return jnp.clip(entries, -bound, bound).astype(kind)


def setup_inputs(seed: int = 0) -> dict:
    seeds = jax.random.split(jax.random.key(seed), 9)
    return {
        "three_index": gaussian(seeds[0], (NOCC, NAUX, NV), 0.18, 1.0, ((0, 128),)),
        "ovl": draw_ovl(jax.random.fold_in(seeds[8], 71), 0),
        "fock_virt": draw_fock_virt(jax.random.fold_in(seeds[8], 71), 0),
        "fock_occ": jnp.clip(jax.random.uniform(seeds[3], (NOCC,), jnp.float32, -1.2, -0.4), -1.2, -0.4),
        "pair_partner": draw_pair_partner(jax.random.fold_in(seeds[8], 71), 0),
        "coup_pair": draw_coup_pair(jax.random.fold_in(seeds[8], 71), 0),
        "coup_fock": gaussian(seeds[6], (NPAIRS, COUP), 0.3, 1.2, ((0, 128),), jnp.float32),
        "dom_blocks": place_ends(jax.random.randint(seeds[7], (NPAIRS,), 1, 3), jax.random.fold_in(seeds[7], 1), 1, 2).astype(jnp.int32),
    }


def reference(three_index, ovl, fock_virt, fock_occ, pair_partner, coup_pair, coup_fock, dom_blocks):
    npairs = NOCC * PAIR_DEV
    first_orb = (jnp.arange(npairs) // PAIR_DEV).astype(jnp.int32)
    second = pair_partner.reshape(-1).astype(jnp.int32)
    virt_diag = jnp.diagonal(fock_virt).astype(jnp.float32)
    shift_occ = fock_occ[first_orb] + fock_occ[second]
    domain_size = dom_blocks * (NV // 2)
    pair_ids = jnp.arange(npairs, dtype=jnp.int32)

    def domain_terms(pair_index):
        inside = jnp.arange(NV) < domain_size[pair_index]
        domain_mask = (inside[:, None] & inside[None, :]).astype(jnp.float32)
        denominator = virt_diag[:, None] + virt_diag[None, :] - shift_occ[pair_index]
        return domain_mask, denominator

    def initial_pair(pair_index):
        integral = jnp.dot(three_index[first_orb[pair_index]].T, three_index[second[pair_index]], preferred_element_type=jnp.float32)
        domain_mask, denominator = domain_terms(pair_index)
        integral = domain_mask * integral
        return integral, (-integral / denominator).astype(jnp.bfloat16)

    pair_int, amplitudes = lax.map(initial_pair, pair_ids)
    residual_out = jnp.zeros(pair_int.shape, jnp.float32)
    for sweep in range(ITERS):
        def update(pair_index):
            current = amplitudes[pair_index]
            coupled_terms = amplitudes[coup_pair[pair_index]].astype(jnp.float32)
            coupled = jnp.sum(coup_fock[pair_index][:, None, None] * coupled_terms, axis=0).astype(jnp.bfloat16)
            right_ovl = jnp.dot(current, ovl, preferred_element_type=jnp.float32).astype(jnp.bfloat16)
            left_ovl = jnp.dot(ovl, current, preferred_element_type=jnp.float32).astype(jnp.bfloat16)
            coupled_ovl = jnp.dot(coupled, ovl, preferred_element_type=jnp.float32).astype(jnp.bfloat16)
            resid_pair = pair_int[pair_index] + jnp.dot(fock_virt, right_ovl, preferred_element_type=jnp.float32)
            resid_pair = resid_pair + jnp.dot(left_ovl, fock_virt, preferred_element_type=jnp.float32)
            resid_pair = resid_pair - shift_occ[pair_index] * jnp.dot(ovl, right_ovl, preferred_element_type=jnp.float32)
            resid_pair = resid_pair - jnp.dot(ovl, coupled_ovl, preferred_element_type=jnp.float32)
            domain_mask, denominator = domain_terms(pair_index)
            masked = domain_mask * resid_pair
            updated = (current.astype(jnp.float32) - masked / denominator).astype(jnp.bfloat16)
            return updated, masked

        amplitudes, residual_out = lax.map(update, pair_ids)
    energy = jnp.sum(pair_int * amplitudes.astype(jnp.float32), axis=(1, 2))
    return amplitudes, residual_out, energy
```

```python
import jax
import jax.numpy as jnp
from jax import lax
from jax.experimental import pallas as pl
from jax.experimental.pallas import tpu as pltpu
from jax.sharding import PartitionSpec as P

ITERS = 2
REACH = 8
OFFSETS = (4, -4, 5, -5, 2, -2, 3, -3, 6, -6, 7, -7, 8, -8, 1, -1)


def shift(block, distance):
    n = lax.axis_size("orb")
    route = [(i, i + distance) for i in range(n) if 0 <= i + distance < n]
    return lax.ppermute(block, "orb", route)


def swap_cores(block):
    n = lax.axis_size("orb")
    return lax.ppermute(block, "orb", [(i, i ^ 1) for i in range(n)])


def domain_mask(size, shape):
    row = lax.broadcasted_iota(jnp.int32, shape, 0)
    col = lax.broadcasted_iota(jnp.int32, shape, 1)
    return (row < size) & (col < size)


def mm(a, b):
    return jnp.dot(a, b, preferred_element_type=jnp.float32)


def send_out(wanted_ref, pair, buf, outs, sem, start):
    for j, out in enumerate(outs):

        @pl.when(wanted_ref[j] == pair)
        def _():
            copy = pltpu.make_async_copy(buf, out, sem.at[j])
            if start:
                copy.start()
            else:
                copy.wait()


def integral_kernel(
    source_ref, wanted_ref, size_ref, shift_ref, at_ref, esum_ref, *rest, nsrc, nout
):
    blocks = rest[:nsrc]
    k_ref, t_ref = rest[nsrc : nsrc + 2]
    outs = rest[nsrc + 2 : nsrc + 2 + nout]
    held, tbuf, in_sem, out_sem = rest[nsrc + 2 + nout :]
    p = pl.program_id(0)
    count = pl.num_programs(0)

    def fetch(pair, start):
        slot = lax.rem(pair, 2)
        for j, block in enumerate(blocks):

            @pl.when(source_ref[pair] == j)
            def _():
                copy = pltpu.make_async_copy(block.at[0], held.at[slot], in_sem.at[slot])
                if start:
                    copy.start()
                else:
                    copy.wait()

    @pl.when(p == 0)
    def _():
        fetch(0, True)

    @pl.when(p + 1 < count)
    def _():
        fetch(p + 1, True)

    fetch(p, False)
    integral = mm(at_ref[...], held[lax.rem(p, 2)])
    mask = domain_mask(size_ref[p], integral.shape)
    integral = jnp.where(mask, integral, 0.0)
    k_ref[0] = integral
    amp = (-integral / (esum_ref[...] - shift_ref[p])).astype(jnp.bfloat16)
    t_ref[0] = amp
    tbuf[p] = amp
    send_out(wanted_ref, p, tbuf.at[p], outs, out_sem, True)

    @pl.when(p == count - 1)
    def _():
        for q in range(tbuf.shape[0]):
            send_out(wanted_ref, q, tbuf.at[q], outs, out_sem, False)


def partial_kernel(shift_ref, k_ref, t_ref, ovl_ref, fock_ref, part_ref):
    p = pl.program_id(0)
    amp = t_ref[0]
    ovl = ovl_ref[...]
    fock = fock_ref[...]
    right = mm(amp, ovl).astype(jnp.bfloat16)
    left = mm(ovl, amp).astype(jnp.bfloat16)
    resid = k_ref[0] + mm(fock, right)
    resid = resid + mm(left, fock)
    part_ref[0] = resid - shift_ref[p] * mm(ovl, right)


def update_kernel(
    source_ref, wanted_ref, size_ref, shift_ref, weight_ref, part_ref, t_ref, esum_ref, ovl_ref,
    *rest, nsrc, nout, last
):
    rest = list(rest)
    k_ref = rest.pop(0) if last else None
    blocks = rest[:nsrc]
    rest = rest[nsrc:]
    tn_ref = rest.pop(0)
    if last:
        resid_ref, energy_ref = rest[:2]
        rest = rest[2:]
        outs = ()
    else:
        outs = rest[:nout]
        rest = rest[nout:]
    held, in_sem = rest[:2]
    p = pl.program_id(0)
    count = pl.num_programs(0)

    def fetch(pair, start):
        slot = lax.rem(pair, 2)
        for c in range(2):
            for j, block in enumerate(blocks):

                @pl.when(source_ref[2 * pair + c] == j)
                def _():
                    copy = pltpu.make_async_copy(block, held.at[slot, c], in_sem.at[slot, c])
                    if start:
                        copy.start()
                    else:
                        copy.wait()

    @pl.when(p == 0)
    def _():
        fetch(0, True)

    @pl.when(p + 1 < count)
    def _():
        fetch(p + 1, True)

    fetch(p, False)
    slot = lax.rem(p, 2)
    first = held[slot, 0].astype(jnp.float32)
    second = held[slot, 1].astype(jnp.float32)
    coupled = (weight_ref[2 * p] * first + weight_ref[2 * p + 1] * second).astype(jnp.bfloat16)
    ovl = ovl_ref[...]
    cross = mm(coupled, ovl).astype(jnp.bfloat16)
    resid = part_ref[0] - mm(ovl, cross)
    resid = jnp.where(domain_mask(size_ref[p], resid.shape), resid, 0.0)
    amp = t_ref[0].astype(jnp.float32) - resid / (esum_ref[...] - shift_ref[p])
    amp = amp.astype(jnp.bfloat16)
    tn_ref[0] = amp
    if last:
        resid_ref[0] = resid
        energy_ref[p] = jnp.sum(k_ref[0] * amp.astype(jnp.float32))
    else:
        tbuf, out_sem = rest[2:]
        tbuf[p] = amp
        send_out(wanted_ref, p, tbuf.at[p], outs, out_sem, True)

        @pl.when(p == count - 1)
        def _():
            for q in range(tbuf.shape[0]):
                send_out(wanted_ref, q, tbuf.at[q], outs, out_sem, False)


ANY = pl.BlockSpec(memory_space=pl.ANY)
SMEM = pl.BlockSpec(memory_space=pltpu.SMEM)


def whole(shape):
    return pl.BlockSpec(shape, lambda p: (0,) * len(shape))


def per_pair(width):
    return pl.BlockSpec((1, width, width), lambda p: (p, 0, 0))


def params():
    return pltpu.CompilerParams(
        dimension_semantics=("arbitrary",), vmem_limit_bytes=48 * 1024 * 1024
    )


def integrals(source, wanted, size, shift_occ, at, esum, blocks):
    pairs = size.shape[0]
    width, aux = at.shape
    f32 = jax.ShapeDtypeStruct((pairs, width, width), jnp.float32)
    b16 = jax.ShapeDtypeStruct((pairs, width, width), jnp.bfloat16)
    one = jax.ShapeDtypeStruct((width, width), jnp.bfloat16)
    nout = len(OFFSETS)

    def body(*refs):
        integral_kernel(*refs, nsrc=len(blocks), nout=nout)

    return pl.pallas_call(
        body,
        grid=(pairs,),
        in_specs=[SMEM] * 4 + [whole(at.shape), whole(esum.shape)] + [ANY] * len(blocks),
        out_specs=[per_pair(width)] * 2 + [ANY] * nout,
        out_shape=[f32, b16] + [one] * nout,
        scratch_shapes=[
            pltpu.VMEM((2, aux, width), jnp.bfloat16),
            pltpu.VMEM((pairs, width, width), jnp.bfloat16),
            pltpu.SemaphoreType.DMA((2,)),
            pltpu.SemaphoreType.DMA((nout,)),
        ],
        compiler_params=params(),
        cost_estimate=pl.CostEstimate(
            flops=2 * pairs * width * width * aux, bytes_accessed=20 << 20, transcendentals=0
        ),
        name="integrals",
    )(source, wanted, size, shift_occ, at, esum, *blocks)


def partial_residual(shift_occ, pair_int, amp, ovl, fock):
    pairs, width, _ = amp.shape
    return pl.pallas_call(
        partial_kernel,
        grid=(pairs,),
        in_specs=[SMEM, per_pair(width), per_pair(width), whole(ovl.shape), whole(fock.shape)],
        out_specs=per_pair(width),
        out_shape=jax.ShapeDtypeStruct(pair_int.shape, jnp.float32),
        compiler_params=params(),
        cost_estimate=pl.CostEstimate(
            flops=10 * pairs * width**3, bytes_accessed=11 << 20, transcendentals=0
        ),
        name="partial",
    )(shift_occ, pair_int, amp, ovl, fock)


def update(source, wanted, size, shift_occ, weight, part, amp, esum, ovl, pair_int, blocks, last):
    pairs, width, _ = amp.shape
    f32 = jax.ShapeDtypeStruct((pairs, width, width), jnp.float32)
    b16 = jax.ShapeDtypeStruct((pairs, width, width), jnp.bfloat16)
    one = jax.ShapeDtypeStruct((width, width), jnp.bfloat16)
    nout = len(OFFSETS)

    def body(*refs):
        update_kernel(*refs, nsrc=len(blocks), nout=nout, last=last)

    operands = [source, wanted, size, shift_occ, weight, part, amp, esum, ovl]
    in_specs = [SMEM] * 5 + [per_pair(width)] * 2 + [whole(esum.shape), whole(ovl.shape)]
    scratch = [
        pltpu.VMEM((2, 2, width, width), jnp.bfloat16),
        pltpu.SemaphoreType.DMA((2, 2)),
    ]
    if last:
        operands.append(pair_int)
        in_specs.append(per_pair(width))
        out_specs = [per_pair(width)] * 2 + [SMEM]
        out_shape = [b16, f32, jax.ShapeDtypeStruct((pairs,), jnp.float32)]
    else:
        out_specs = [per_pair(width)] + [ANY] * nout
        out_shape = [b16] + [one] * nout
        scratch += [
            pltpu.VMEM((pairs, width, width), jnp.bfloat16),
            pltpu.SemaphoreType.DMA((nout,)),
        ]
    return pl.pallas_call(
        body,
        grid=(pairs,),
        in_specs=in_specs + [ANY] * len(blocks),
        out_specs=out_specs,
        out_shape=out_shape,
        scratch_shapes=scratch,
        compiler_params=params(),
        cost_estimate=pl.CostEstimate(
            flops=4 * pairs * width**3, bytes_accessed=20 << 20, transcendentals=0
        ),
        name="update",
    )(*operands, *blocks)


def per_device(
    three_index, ovl, fock_virt, fock_occ, pair_partner, coup_pair, coup_fock, dom_blocks
):
    n = lax.axis_size("orb")
    pairs = pair_partner.shape[1]
    width = ovl.shape[0]
    own = lax.axis_index("orb")
    core = lax.rem(own, 2)

    below2 = shift(three_index, 2)
    above2 = shift(three_index, -2)
    mate = swap_cores(three_index)
    below4 = shift(below2, 2)
    above4 = shift(above2, -2)
    below2_mate = swap_cores(below2)
    above2_mate = swap_cores(above2)
    below3 = lax.ppermute(below4, "orb", [(i, i - 1) for i in range(1, n, 2)])
    above3 = lax.ppermute(above4, "orb", [(i, i + 1) for i in range(0, n, 2)])
    blocks = [below4, below2, below2_mate, mate, above2_mate, above2, above4, below3, above3]

    row = coup_pair.reshape(1, -1)
    other = swap_cores(row)
    both = jnp.where(core == 0, jnp.concatenate([row, other]), jnp.concatenate([other, row]))
    half = REACH // 2
    table = jnp.concatenate(
        [both if d == 0 else shift(both, -2 * d) for d in range(-half, half + 1)]
    )
    table = lax.dynamic_slice(table, (core, 0), (2 * REACH + 1, table.shape[1]))
    wanted = []
    for d in OFFSETS:
        reader = own - d
        line = table[REACH - d]
        code = jnp.sum(jnp.where(line // pairs == own, line % pairs + 1, 0))
        wanted.append(jnp.where((reader >= 0) & (reader < n), code, 0) - 1)
    wanted = jnp.stack(wanted)

    offset = pair_partner[0] - own
    even = {-4: 0, -3: 7, -2: 1, -1: 2, 1: 3, 2: 5, 3: 4, 4: 6}
    odd = {-4: 0, -3: 2, -2: 1, -1: 3, 1: 4, 2: 5, 3: 8, 4: 6}
    source = jnp.zeros((pairs,), jnp.int32)
    for d in even:
        source = jnp.where(offset == d, jnp.where(core == 0, even[d], odd[d]), source)

    relative = coup_pair.reshape(-1) // pairs - own
    origin = jnp.zeros(relative.shape, jnp.int32)
    for j, d in enumerate(OFFSETS):
        origin = jnp.where(relative == d, j, origin)
    weight = coup_fock.reshape(-1)

    size = dom_blocks * (width // 2)
    orbitals = jnp.arange(fock_occ.shape[0])
    shift_occ = jnp.sum(jnp.where(orbitals == own, fock_occ, 0.0)) + jnp.sum(
        jnp.where(orbitals[None, :] == pair_partner[0][:, None], fock_occ[None, :], 0.0), axis=1
    )
    eye = jnp.arange(width)[:, None] == jnp.arange(width)[None, :]
    diag = jnp.where(eye, fock_virt.astype(jnp.float32), 0.0)
    esum = jnp.sum(diag, axis=1)[:, None] + jnp.sum(diag, axis=0)[None, :]
    at = three_index[0].T

    pair_int, amp, *outgoing = integrals(source, wanted, size, shift_occ, at, esum, blocks)
    for sweep in range(ITERS):
        last = sweep == ITERS - 1
        received = [shift(out, -d) for out, d in zip(outgoing, OFFSETS)]
        part = partial_residual(shift_occ, pair_int, amp, ovl, fock_virt)
        amp, *outgoing = update(
            origin, wanted, size, shift_occ, weight, part, amp, esum, ovl, pair_int, received, last
        )
    residual, energy = outgoing
    return amp, residual, energy


def solution(mesh):
    placed = (
        P("orb", None, None),
        P(),
        P(),
        P(),
        P("orb", None),
        P("orb", None),
        P("orb", None),
        P("orb"),
    )
    return jax.shard_map(
        per_device,
        mesh=mesh,
        in_specs=placed,
        out_specs=(P("orb", None, None), P("orb", None, None), P("orb")),
        check_vma=False,
    )
```

```python
import jax
import jax.numpy as jnp
from jax import lax
from jax.experimental import pallas as pl
from jax.experimental.pallas import tpu as pltpu
from jax.sharding import PartitionSpec as P


ITERS = 2
REACH = 8
HEAD = 16
OFFSETS = (4, -4, 8, -8, 3, -3, 7, -7, 5, -5, 6, -6, 2, -2, 1, -1)
EVEN = {-4: 0, -3: 7, -2: 1, -1: 2, 1: 3, 2: 5, 3: 4, 4: 6}
ODD = {-4: 0, -3: 2, -2: 1, -1: 3, 1: 4, 2: 5, 3: 8, 4: 6}


def shift(block, distance, cyclic=False):
    n = lax.axis_size("orb")
    route = [(i, (i + distance) % n) for i in range(n) if cyclic or 0 <= i + distance < n]
    return lax.ppermute(block, "orb", route)


def in_hbm(block):
    return pltpu.with_memory_space_constraint(block, pltpu.HBM)


def swap_cores(block):
    n = lax.axis_size("orb")
    return lax.ppermute(block, "orb", [(i, i ^ 1) for i in range(n)])


def domain_mask(size, shape):
    row = lax.broadcasted_iota(jnp.int32, shape, 0)
    col = lax.broadcasted_iota(jnp.int32, shape, 1)
    return (row < size) & (col < size)


def mm(a, b):
    return jnp.dot(a, b, preferred_element_type=jnp.float32)


def occupied_shift(own, partner_ref, occ_ref, pair):
    return occ_ref[own] + occ_ref[partner_ref[0, pair]]


def send_pair(own, code_ref, pair, buf, outs, sem):
    base = REACH + lax.rem(own, 2)
    for j, out in enumerate(outs):

        @pl.when(code_ref[base - OFFSETS[j]] == pair)
        def _():
            pltpu.make_async_copy(buf, out, sem.at[j]).start()


def finish_sends(own, code_ref, buf, outs, sem):
    base = REACH + lax.rem(own, 2)
    for j, out in enumerate(outs):

        @pl.when(code_ref[base - OFFSETS[j]] >= 0)
        def _():
            pltpu.make_async_copy(buf, out, sem.at[j]).wait()


def integral_kernel(own_ref, partner_ref, code_ref, dom_ref, occ_ref, at_ref, esum_ref, *rest):
    blocks = rest[:9]
    k_out, t_out = rest[9:11]
    outs = rest[11:-6]
    held, k_ref, t_ref, in_sem, out_sem, keep_sem = rest[-6:]
    own = own_ref[0]
    pairs, aux, width = held.shape

    def fetch(pair):
        offset = partner_ref[0, pair] - own
        even = lax.rem(own, 2) == 0
        for j, block in enumerate(blocks):
            match = jnp.zeros((), jnp.bool_)
            for d in EVEN:
                if EVEN[d] == j:
                    match = match | (even & (offset == d))
                if ODD[d] == j:
                    match = match | (~even & (offset == d))

            @pl.when(match)
            def _():
                pltpu.make_async_copy(
                    block.at[pl.ds(0, aux)], held.at[pair], in_sem.at[pair]
                ).start()

    def keep(pair):
        return (
            pltpu.make_async_copy(k_ref.at[pair], k_out.at[pair], keep_sem.at[2 * pair]),
            pltpu.make_async_copy(t_ref.at[pair], t_out.at[pair], keep_sem.at[2 * pair + 1]),
        )

    for pair in range(pairs):
        fetch(pair)
    for pair in range(pairs):
        pltpu.make_async_copy(
            blocks[0].at[pl.ds(0, aux)], held.at[pair], in_sem.at[pair]
        ).wait()
        integral = mm(at_ref[...], held[pair])
        mask = domain_mask(dom_ref[pair] * (width // 2), integral.shape)
        integral = jnp.where(mask, integral, 0.0)
        k_ref[pair] = integral
        denominator = esum_ref[...] - occupied_shift(own, partner_ref, occ_ref, pair)
        t_ref[pair] = (-integral / denominator).astype(jnp.bfloat16)
        send_pair(own, code_ref, pair, t_ref.at[pair], outs, out_sem)
        for copy in keep(pair):
            copy.start()
    finish_sends(own, code_ref, t_ref.at[0], outs, out_sem)
    for pair in range(pairs):
        for copy in keep(pair):
            copy.wait()


def partial_kernel(
    own_ref, partner_ref, occ_ref, dom_ref, k_ref, t_ref, ovl_ref, fock_ref, esum_ref,
    gain_ref, base_ref, part_ref=None
):
    own = own_ref[0]
    ovl = ovl_ref[...]
    fock = fock_ref[...]

    def step(pair, _):
        amp = t_ref[pair]
        right = mm(amp, ovl).astype(jnp.bfloat16)
        left = mm(ovl, amp).astype(jnp.bfloat16)
        resid = k_ref[pair] + mm(fock, right)
        resid = resid + mm(left, fock)
        shift_occ = occupied_shift(own, partner_ref, occ_ref, pair)
        resid = resid - shift_occ * mm(ovl, right)
        mask = domain_mask(dom_ref[pair] * (amp.shape[0] // 2), amp.shape)
        gain = jnp.where(mask, 1.0 / (esum_ref[...] - shift_occ), 0.0)
        gain_ref[pair] = gain
        base_ref[pair] = amp.astype(jnp.float32) - resid * gain
        if part_ref is not None:
            part_ref[pair] = jnp.where(mask, resid, 0.0)
        return 0

    lax.fori_loop(0, t_ref.shape[0], step, 0)


def update_kernel(
    own_ref, code_ref, place_ref, weight_ref, dom_ref, gain_ref, base_ref, ovl_ref, *rest, last
):
    rest = list(rest)
    if last:
        part_ref, k_ref = rest[:2]
        rest = rest[2:]
    blocks = rest[: len(OFFSETS)]
    rest = rest[len(OFFSETS) :]
    if last:
        tn_ref, resid_ref, energy_ref, held, in_sem, out_sem, tbuf, rbuf = rest
    else:
        tn_ref = rest[0]
        outs = rest[1:-3]
        held, in_sem, out_sem = rest[-3:]
    own = own_ref[0]
    pairs, width, _ = base_ref.shape

    middle = REACH + lax.rem(own, 2)
    for j, block in enumerate(blocks):
        entry = place_ref[middle + OFFSETS[j]]

        @pl.when(entry >= 0)
        def _():
            pltpu.make_async_copy(block, held.at[entry], in_sem.at[entry]).start()

    def results(pair):
        return (
            pltpu.make_async_copy(tbuf.at[pair], tn_ref.at[pair], out_sem.at[2 * pair]),
            pltpu.make_async_copy(rbuf.at[pair], resid_ref.at[pair], out_sem.at[2 * pair + 1]),
        )

    ovl = ovl_ref[...]
    for pair in range(pairs):
        for entry in (2 * pair, 2 * pair + 1):
            pltpu.make_async_copy(blocks[0], held.at[entry], in_sem.at[entry]).wait()
        first = held[2 * pair].astype(jnp.float32)
        second = held[2 * pair + 1].astype(jnp.float32)
        coupled = weight_ref[pair, 0] * first + weight_ref[pair, 1] * second
        cross = mm(coupled.astype(jnp.bfloat16), ovl).astype(jnp.bfloat16)
        term = mm(ovl, cross)
        amp = (base_ref[pair] + term * gain_ref[pair]).astype(jnp.bfloat16)
        if last:
            tbuf[pair] = amp
            mask = domain_mask(dom_ref[pair] * (width // 2), term.shape)
            rbuf[pair] = part_ref[pair] - jnp.where(mask, term, 0.0)
            for copy in results(pair):
                copy.start()
            energy_ref[pair] = jnp.sum(k_ref[pair] * amp.astype(jnp.float32))
        else:
            tn_ref[pair] = amp
            send_pair(own, code_ref, pair, tn_ref.at[pair], outs, out_sem)
    if last:
        for pair in range(pairs):
            for copy in results(pair):
                copy.wait()
    else:
        finish_sends(own, code_ref, tn_ref.at[0], outs, out_sem)


ANY = pl.BlockSpec(memory_space=pl.ANY)
SMEM = pl.BlockSpec(memory_space=pltpu.SMEM)
VMEM = pl.BlockSpec(memory_space=pltpu.VMEM)
HBM = pl.BlockSpec(memory_space=pltpu.HBM)


def params(mib):
    return pltpu.CompilerParams(vmem_limit_bytes=mib * 1024 * 1024)


def cost(flops, mib):
    return pl.CostEstimate(flops=flops, bytes_accessed=mib << 20, transcendentals=0)


def integrals(own, partner, code, dom, occ, at, esum, blocks):
    pairs = dom.shape[0]
    width, aux = at.shape
    nout = len(OFFSETS)
    one = jax.ShapeDtypeStruct((width, width), jnp.bfloat16)
    return pl.pallas_call(
        integral_kernel,
        in_specs=[SMEM] * 5 + [VMEM] * 2 + [ANY] * len(blocks),
        out_specs=[HBM] * 2 + [ANY] * nout,
        out_shape=[
            pltpu.HBM((pairs, width, width), jnp.float32),
            pltpu.HBM((pairs, width, width), jnp.bfloat16),
        ]
        + [one] * nout,
        scratch_shapes=[
            pltpu.VMEM((pairs, aux, width), jnp.bfloat16),
            pltpu.VMEM((pairs, width, width), jnp.float32),
            pltpu.VMEM((pairs, width, width), jnp.bfloat16),
            pltpu.SemaphoreType.DMA((pairs,)),
            pltpu.SemaphoreType.DMA((nout,)),
            pltpu.SemaphoreType.DMA((2 * pairs,)),
        ],
        compiler_params=params(16),
        cost_estimate=cost(2 * pairs * width * width * aux, 20),
        name="integrals",
    )(own, partner, code, dom, occ, at, esum, *blocks)


def partial_residual(own, partner, occ, dom, pair_int, amp, ovl, fock, esum, last):
    pairs, width, _ = amp.shape
    f32 = jax.ShapeDtypeStruct(pair_int.shape, jnp.float32)
    return pl.pallas_call(
        partial_kernel,
        in_specs=[SMEM] * 4 + [VMEM] * 5,
        out_specs=[VMEM] * (3 if last else 2),
        out_shape=[f32] * (3 if last else 2),
        compiler_params=params(20),
        cost_estimate=cost(10 * pairs * width**3, 20),
        name="partial",
    )(own, partner, occ, dom, pair_int, amp, ovl, fock, esum)


def update(own, code, place, weight, dom, terms, ovl, pair_int, blocks, last):
    pairs, width, _ = pair_int.shape
    f32 = jax.ShapeDtypeStruct((pairs, width, width), jnp.float32)
    b16 = jax.ShapeDtypeStruct((pairs, width, width), jnp.bfloat16)
    one = jax.ShapeDtypeStruct((width, width), jnp.bfloat16)
    nout = len(OFFSETS)

    def body(*refs):
        update_kernel(*refs, last=last)

    operands = [own, code, place, weight, dom, *terms[:2], ovl]
    scratch = [
        pltpu.VMEM((2 * pairs, width, width), jnp.bfloat16),
        pltpu.SemaphoreType.DMA((2 * pairs,)),
    ]
    if last:
        operands += [terms[2], pair_int]
        out_specs = [HBM] * 2 + [SMEM]
        out_shape = [b16, f32, jax.ShapeDtypeStruct((pairs,), jnp.float32)]
        scratch += [
            pltpu.SemaphoreType.DMA((2 * pairs,)),
            pltpu.VMEM(b16.shape, b16.dtype),
            pltpu.VMEM(f32.shape, f32.dtype),
        ]
    else:
        out_specs = [VMEM] + [ANY] * nout
        out_shape = [b16] + [one] * nout
        scratch += [pltpu.SemaphoreType.DMA((nout,))]
    return pl.pallas_call(
        body,
        in_specs=[SMEM] * 5 + [VMEM] * (len(operands) - 5) + [ANY] * len(blocks),
        out_specs=out_specs,
        out_shape=out_shape,
        scratch_shapes=scratch,
        compiler_params=params(20),
        cost_estimate=cost(4 * pairs * width**3, 20),
        name="update",
    )(*operands, *blocks)


def coupling_table(core, chips):
    rows = jnp.concatenate(
        [
            jnp.where(core == 0, jnp.stack([a, b]), jnp.stack([b, a])).reshape(2, -1)
            for a, b in chips
        ]
    )
    return jnp.concatenate([shift(rows, 6, True), rows, shift(rows, -6, True)])


def coupling_codes(own, core, table, listed_owner):
    table = table.astype(jnp.int32)
    half = table.shape[1] // 2
    owners, slots = table[:, :half], table[:, half:]
    code = jnp.sum(jnp.where(owners == own, slots + 1, 0), axis=1)
    orbital = own - core - REACH + jnp.arange(code.shape[0])
    code = jnp.where((orbital >= 0) & (orbital < lax.axis_size("orb")), code, 0) - 1
    position = jnp.where(listed_owner[None, :] == orbital[:, None], jnp.arange(1, half + 1), 0)
    return code, jnp.sum(position, axis=1) - 1


def per_device(
    three_index, ovl, fock_virt, fock_occ, pair_partner, coup_pair, coup_fock, dom_blocks
):
    n = lax.axis_size("orb")
    pairs = pair_partner.shape[1]
    aux, width = three_index.shape[1:]
    own = lax.axis_index("orb")
    core = lax.rem(own, 2)

    listed = coup_pair.reshape(-1)
    head = jnp.stack([listed // pairs, listed % pairs]).astype(jnp.bfloat16)
    entries = head.shape[1]
    block = jnp.concatenate(
        [three_index[0], jnp.pad(head, ((0, HEAD - 2), (0, width - entries)))]
    )
    below2 = shift(block, 2, True)
    above2 = shift(block, -2, True)
    mate = swap_cores(block)
    eye = jnp.arange(width)[:, None] == jnp.arange(width)[None, :]
    diag = jnp.where(eye, fock_virt.astype(jnp.float32), 0.0)
    esum = jnp.sum(diag, axis=1)[:, None] + jnp.sum(diag, axis=0)[None, :]
    at = three_index[0].T
    below4 = shift(below2, 2)
    above4 = shift(above2, -2)
    below2_mate = swap_cores(below2)
    above2_mate = swap_cores(above2)

    def header(x):
        return x[aux : aux + 2, :entries]

    table = coupling_table(
        core,
        [
            (header(below2), header(below2_mate)),
            (head, header(mate)),
            (header(above2), header(above2_mate)),
        ],
    )
    code, place = coupling_codes(own, core, table, listed // pairs)
    below3 = lax.ppermute(below4, "orb", [(i, i - 1) for i in range(1, n, 2)])
    above3 = lax.ppermute(above4, "orb", [(i, i + 1) for i in range(0, n, 2)])
    blocks = [below4, below2, below2_mate, mate, above2_mate, above2, above4, below3, above3]
    blocks = [in_hbm(b) for b in blocks]

    own1 = own.reshape(1)

    pair_int, amp, *outgoing = integrals(
        own1, pair_partner, code, dom_blocks, fock_occ, at, esum, blocks
    )
    for sweep in range(ITERS):
        last = sweep == ITERS - 1
        received = [shift(out, -d) for out, d in zip(outgoing, OFFSETS)]
        terms = partial_residual(
            own1, pair_partner, fock_occ, dom_blocks, pair_int, amp, ovl, fock_virt, esum, last
        )
        amp, *outgoing = update(
            own1, code, place, coup_fock, dom_blocks, terms, ovl, pair_int, received, last
        )
    residual, energy = outgoing
    return amp, residual, energy


def solution(mesh):
    placed = (
        P("orb", None, None),
        P(),
        P(),
        P(),
        P("orb", None),
        P("orb", None),
        P("orb", None),
        P("orb"),
    )

    return jax.shard_map(
        per_device,
        mesh=mesh,
        in_specs=placed,
        out_specs=(P("orb", None, None), P("orb", None, None), P("orb")),
        check_vma=False,
    )
```

```python
import jax
import jax.numpy as jnp
from jax import lax
from jax.experimental import pallas as pl
from jax.experimental.pallas import tpu as pltpu
from jax.sharding import PartitionSpec as P


ITERS = 2
REACH = 8
HEAD = 16
OFFSETS = (-4, 4, -8, 8, -3, 3, -7, 7, -5, 5, -6, 6, -2, 2, -1, 1)
EVEN = {-4: 0, -3: 7, -2: 1, -1: 2, 1: 3, 2: 5, 3: 4, 4: 6}
ODD = {-4: 0, -3: 2, -2: 1, -1: 3, 1: 4, 2: 5, 3: 8, 4: 6}


def shift(block, distance, cyclic=False):
    n = lax.axis_size("orb")
    route = [(i, (i + distance) % n) for i in range(n) if cyclic or 0 <= i + distance < n]
    return lax.ppermute(block, "orb", route)


def in_hbm(block):
    return pltpu.with_memory_space_constraint(block, pltpu.HBM)


def swap_cores(block):
    n = lax.axis_size("orb")
    return lax.ppermute(block, "orb", [(i, i ^ 1) for i in range(n)])


def domain_mask(size, shape):
    row = lax.broadcasted_iota(jnp.int32, shape, 0)
    col = lax.broadcasted_iota(jnp.int32, shape, 1)
    return (row < size) & (col < size)


def mm(a, b):
    return jnp.dot(a, b, preferred_element_type=jnp.float32)


def occupied_shift(own, partner_ref, occ_ref, pair):
    return occ_ref[own] + occ_ref[partner_ref[0, pair]]


def send_pair(own, code_ref, pair, buf, outs, sem):
    base = REACH + lax.rem(own, 2)
    for j, out in enumerate(outs):

        @pl.when(code_ref[base - OFFSETS[j]] == pair)
        def _():
            pltpu.make_async_copy(buf, out, sem.at[j]).start()


def finish_sends(own, code_ref, buf, outs, sem):
    base = REACH + lax.rem(own, 2)
    for j, out in enumerate(outs):

        @pl.when(code_ref[base - OFFSETS[j]] >= 0)
        def _():
            pltpu.make_async_copy(buf, out, sem.at[j]).wait()


def integral_kernel(own_ref, partner_ref, code_ref, dom_ref, occ_ref, at_ref, esum_ref, *rest):
    count = len(rest) - 8 - len(OFFSETS)
    blocks = rest[:count]
    k_out, t_out = rest[count : count + 2]
    outs = rest[count + 2 : -6]
    held, k_ref, t_ref, in_sem, out_sem, keep_sem = rest[-6:]
    own = own_ref[0]
    pairs, aux, width = held.shape
    cut = aux // 2

    def fetch(pair):
        offset = partner_ref[0, pair] - own
        even = lax.rem(own, 2) == 0
        for j, (block_a, block_b) in enumerate(zip(blocks[: count // 2], blocks[count // 2 :])):
            match = jnp.zeros((), jnp.bool_)
            for d in EVEN:
                if EVEN[d] == j:
                    match = match | (even & (offset == d))
                if ODD[d] == j:
                    match = match | (~even & (offset == d))

            @pl.when(match)
            def _():
                pltpu.make_async_copy(
                    block_a, held.at[pair, pl.ds(0, cut)], in_sem.at[pair, 0]
                ).start()
                pltpu.make_async_copy(
                    block_b.at[pl.ds(0, cut)], held.at[pair, pl.ds(cut, cut)], in_sem.at[pair, 1]
                ).start()

    def keep(pair):
        return (
            pltpu.make_async_copy(k_ref.at[pair], k_out.at[pair], keep_sem.at[2 * pair]),
            pltpu.make_async_copy(t_ref.at[pair], t_out.at[pair], keep_sem.at[2 * pair + 1]),
        )

    for pair in range(pairs):
        fetch(pair)
    for pair in range(pairs):
        for h in range(2):
            pltpu.make_async_copy(
                blocks[0], held.at[pair, pl.ds(h * cut, cut)], in_sem.at[pair, h]
            ).wait()
        integral = mm(at_ref[...], held[pair])
        mask = domain_mask(dom_ref[pair] * (width // 2), integral.shape)
        integral = jnp.where(mask, integral, 0.0)
        k_ref[pair] = integral
        denominator = esum_ref[...] - occupied_shift(own, partner_ref, occ_ref, pair)
        t_ref[pair] = (-integral / denominator).astype(jnp.bfloat16)
        send_pair(own, code_ref, pair, t_ref.at[pair], outs, out_sem)
        for copy in keep(pair):
            copy.start()
    finish_sends(own, code_ref, t_ref.at[0], outs, out_sem)
    for pair in range(pairs):
        for copy in keep(pair):
            copy.wait()


def partial_kernel(
    own_ref, partner_ref, occ_ref, dom_ref, k_ref, t_ref, ovl_ref, fock_ref, esum_ref,
    gain_ref, base_ref, part_ref=None
):
    own = own_ref[0]
    ovl = ovl_ref[...]
    fock = fock_ref[...]

    def step(pair, _):
        amp = t_ref[pair]
        right = mm(amp, ovl).astype(jnp.bfloat16)
        left = mm(ovl, amp).astype(jnp.bfloat16)
        resid = k_ref[pair] + mm(fock, right)
        resid = resid + mm(left, fock)
        shift_occ = occupied_shift(own, partner_ref, occ_ref, pair)
        resid = resid - shift_occ * mm(ovl, right)
        mask = domain_mask(dom_ref[pair] * (amp.shape[0] // 2), amp.shape)
        gain = jnp.where(mask, 1.0 / (esum_ref[...] - shift_occ), 0.0)
        gain_ref[pair] = gain
        base_ref[pair] = amp.astype(jnp.float32) - resid * gain
        if part_ref is not None:
            part_ref[pair] = jnp.where(mask, resid, 0.0)
        return 0

    lax.fori_loop(0, t_ref.shape[0], step, 0)


def update_kernel(
    own_ref, code_ref, place_ref, weight_ref, dom_ref, gain_ref, base_ref, ovl_ref, *rest, last
):
    rest = list(rest)
    if last:
        part_ref, k_ref = rest[:2]
        rest = rest[2:]
    blocks = rest[: len(OFFSETS)]
    rest = rest[len(OFFSETS) :]
    if last:
        tn_ref, resid_ref, energy_ref, held, in_sem, out_sem, tbuf, rbuf = rest
    else:
        tn_ref = rest[0]
        outs = rest[1:-3]
        held, in_sem, out_sem = rest[-3:]
    own = own_ref[0]
    pairs, width, _ = base_ref.shape

    middle = REACH + lax.rem(own, 2)
    for j, block in enumerate(blocks):
        entry = place_ref[middle + OFFSETS[j]]

        @pl.when(entry >= 0)
        def _():
            pltpu.make_async_copy(block, held.at[entry], in_sem.at[entry]).start()

    def results(pair):
        return (
            pltpu.make_async_copy(tbuf.at[pair], tn_ref.at[pair], out_sem.at[2 * pair]),
            pltpu.make_async_copy(rbuf.at[pair], resid_ref.at[pair], out_sem.at[2 * pair + 1]),
        )

    ovl = ovl_ref[...]
    for pair in range(pairs):
        for entry in (2 * pair, 2 * pair + 1):
            pltpu.make_async_copy(blocks[0], held.at[entry], in_sem.at[entry]).wait()
        first = held[2 * pair].astype(jnp.float32)
        second = held[2 * pair + 1].astype(jnp.float32)
        coupled = weight_ref[pair, 0] * first + weight_ref[pair, 1] * second
        cross = mm(coupled.astype(jnp.bfloat16), ovl).astype(jnp.bfloat16)
        term = mm(ovl, cross)
        amp = (base_ref[pair] + term * gain_ref[pair]).astype(jnp.bfloat16)
        if last:
            tbuf[pair] = amp
            mask = domain_mask(dom_ref[pair] * (width // 2), term.shape)
            rbuf[pair] = part_ref[pair] - jnp.where(mask, term, 0.0)
            for copy in results(pair):
                copy.start()
            energy_ref[pair] = jnp.sum(k_ref[pair] * amp.astype(jnp.float32))
        else:
            tn_ref[pair] = amp
            send_pair(own, code_ref, pair, tn_ref.at[pair], outs, out_sem)
    if last:
        for pair in range(pairs):
            for copy in results(pair):
                copy.wait()
    else:
        finish_sends(own, code_ref, tn_ref.at[0], outs, out_sem)


ANY = pl.BlockSpec(memory_space=pl.ANY)
SMEM = pl.BlockSpec(memory_space=pltpu.SMEM)
VMEM = pl.BlockSpec(memory_space=pltpu.VMEM)
HBM = pl.BlockSpec(memory_space=pltpu.HBM)


def params(mib):
    return pltpu.CompilerParams(vmem_limit_bytes=mib * 1024 * 1024)


def cost(flops, mib):
    return pl.CostEstimate(flops=flops, bytes_accessed=mib << 20, transcendentals=0)


def integrals(own, partner, code, dom, occ, at, esum, blocks):
    pairs = dom.shape[0]
    width, aux = at.shape
    nout = len(OFFSETS)
    one = jax.ShapeDtypeStruct((width, width), jnp.bfloat16)
    return pl.pallas_call(
        integral_kernel,
        in_specs=[SMEM] * 5 + [VMEM] * 2 + [ANY] * len(blocks),
        out_specs=[HBM] * 2 + [ANY] * nout,
        out_shape=[
            pltpu.HBM((pairs, width, width), jnp.float32),
            pltpu.HBM((pairs, width, width), jnp.bfloat16),
        ]
        + [one] * nout,
        scratch_shapes=[
            pltpu.VMEM((pairs, aux, width), jnp.bfloat16),
            pltpu.VMEM((pairs, width, width), jnp.float32),
            pltpu.VMEM((pairs, width, width), jnp.bfloat16),
            pltpu.SemaphoreType.DMA((pairs, 2)),
            pltpu.SemaphoreType.DMA((nout,)),
            pltpu.SemaphoreType.DMA((2 * pairs,)),
        ],
        compiler_params=params(16),
        cost_estimate=cost(2 * pairs * width * width * aux, 20),
        name="integrals",
    )(own, partner, code, dom, occ, at, esum, *blocks)


def partial_residual(own, partner, occ, dom, pair_int, amp, ovl, fock, esum, last):
    pairs, width, _ = amp.shape
    f32 = jax.ShapeDtypeStruct(pair_int.shape, jnp.float32)
    return pl.pallas_call(
        partial_kernel,
        in_specs=[SMEM] * 4 + [VMEM] * 5,
        out_specs=[VMEM] * (3 if last else 2),
        out_shape=[f32] * (3 if last else 2),
        compiler_params=params(20),
        cost_estimate=cost(10 * pairs * width**3, 20),
        name="partial",
    )(own, partner, occ, dom, pair_int, amp, ovl, fock, esum)


def update(own, code, place, weight, dom, terms, ovl, pair_int, blocks, last):
    pairs, width, _ = pair_int.shape
    f32 = jax.ShapeDtypeStruct((pairs, width, width), jnp.float32)
    b16 = jax.ShapeDtypeStruct((pairs, width, width), jnp.bfloat16)
    one = jax.ShapeDtypeStruct((width, width), jnp.bfloat16)
    nout = len(OFFSETS)

    def body(*refs):
        update_kernel(*refs, last=last)

    operands = [own, code, place, weight, dom, *terms[:2], ovl]
    scratch = [
        pltpu.VMEM((2 * pairs, width, width), jnp.bfloat16),
        pltpu.SemaphoreType.DMA((2 * pairs,)),
    ]
    if last:
        operands += [terms[2], pair_int]
        out_specs = [HBM] * 2 + [SMEM]
        out_shape = [b16, f32, jax.ShapeDtypeStruct((pairs,), jnp.float32)]
        scratch += [
            pltpu.SemaphoreType.DMA((2 * pairs,)),
            pltpu.VMEM(b16.shape, b16.dtype),
            pltpu.VMEM(f32.shape, f32.dtype),
        ]
    else:
        out_specs = [VMEM] + [ANY] * nout
        out_shape = [b16] + [one] * nout
        scratch += [pltpu.SemaphoreType.DMA((nout,))]
    return pl.pallas_call(
        body,
        in_specs=[SMEM] * 5 + [VMEM] * (len(operands) - 5) + [ANY] * len(blocks),
        out_specs=out_specs,
        out_shape=out_shape,
        scratch_shapes=scratch,
        compiler_params=params(20),
        cost_estimate=cost(4 * pairs * width**3, 20),
        name="update",
    )(*operands, *blocks)


def coupling_table(core, chips):
    rows = jnp.concatenate(
        [
            jnp.where(core == 0, jnp.stack([a, b]), jnp.stack([b, a])).reshape(2, -1)
            for a, b in chips
        ]
    )
    lower, upper = shift(rows, 6, True), shift(rows, -6, True)
    return jnp.concatenate([lower, rows, upper])


def coupling_codes(own, core, table, listed_owner):
    table = table.astype(jnp.int32)
    half = table.shape[1] // 2
    owners, slots = table[:, :half], table[:, half:]
    code = jnp.sum(jnp.where(owners == own, slots + 1, 0), axis=1)
    orbital = own - core - REACH + jnp.arange(code.shape[0])
    code = jnp.where((orbital >= 0) & (orbital < lax.axis_size("orb")), code, 0) - 1
    position = jnp.where(listed_owner[None, :] == orbital[:, None], jnp.arange(1, half + 1), 0)
    return code, jnp.sum(position, axis=1) - 1


def window(block):
    n = lax.axis_size("orb")
    below2 = shift(block, 2, True)
    above2 = shift(block, -2, True)
    mate = swap_cores(block)
    below4 = shift(below2, 2)
    above4 = shift(above2, -2)
    below2_mate = swap_cores(below2)
    above2_mate = swap_cores(above2)
    below3 = lax.ppermute(below4, "orb", [(i, i - 1) for i in range(1, n, 2)])
    above3 = lax.ppermute(above4, "orb", [(i, i + 1) for i in range(0, n, 2)])
    return [below4, below2, below2_mate, mate, above2_mate, above2, above4, below3, above3]


def per_device(
    three_index, ovl, fock_virt, fock_occ, pair_partner, coup_pair, coup_fock, dom_blocks
):
    pairs = pair_partner.shape[1]
    aux, width = three_index.shape[1:]
    own = lax.axis_index("orb")
    core = lax.rem(own, 2)

    listed = coup_pair.reshape(-1)
    head = jnp.stack([listed // pairs, listed % pairs]).astype(jnp.bfloat16)
    entries = head.shape[1]
    cut = aux // 2
    block_a = three_index[0, :cut]
    block_b = jnp.concatenate(
        [three_index[0, cut:], jnp.pad(head, ((0, HEAD - 2), (0, width - entries)))]
    )
    eye = jnp.arange(width)[:, None] == jnp.arange(width)[None, :]
    diag = jnp.where(eye, fock_virt.astype(jnp.float32), 0.0)
    esum = jnp.sum(diag, axis=1)[:, None] + jnp.sum(diag, axis=0)[None, :]
    at = three_index[0].T
    blocks_a = window(block_a)
    blocks_b = window(block_b)
    _, below2, below2_mate, mate, above2_mate, above2 = blocks_b[:6]

    def header(x):
        return x[aux - cut : aux - cut + 2, :entries]

    table = coupling_table(
        core,
        [
            (header(below2), header(below2_mate)),
            (head, header(mate)),
            (header(above2), header(above2_mate)),
        ],
    )
    code, place = coupling_codes(own, core, table, listed // pairs)
    blocks = [in_hbm(b) for b in blocks_a + blocks_b[:7]] + blocks_b[7:]

    own1 = own.reshape(1)

    pair_int, amp, *outgoing = integrals(
        own1, pair_partner, code, dom_blocks, fock_occ, at, esum, blocks
    )
    for sweep in range(ITERS):
        last = sweep == ITERS - 1
        received = [shift(out, -d) for out, d in zip(outgoing, OFFSETS)]
        terms = partial_residual(
            own1, pair_partner, fock_occ, dom_blocks, pair_int, amp, ovl, fock_virt, esum, last
        )
        amp, *outgoing = update(
            own1, code, place, coup_fock, dom_blocks, terms, ovl, pair_int, received, last
        )
    residual, energy = outgoing
    return amp, residual, energy


def solution(mesh):
    placed = (
        P("orb", None, None),
        P(),
        P(),
        P(),
        P("orb", None),
        P("orb", None),
        P("orb", None),
        P("orb"),
    )

    return jax.shard_map(
        per_device,
        mesh=mesh,
        in_specs=placed,
        out_specs=(P("orb", None, None), P("orb", None, None), P("orb")),
        check_vma=False,
    )
```
